32 devices in a mesh: pipe: 4 (over y, x), row: 4 (over z), col: 2 (over core).
Axes of the slice: x: 2, y: 2, z: 4, core: 2. Of those that a mesh axis runs over, the one named last changes fastest.
Arguments:
- acts: bfloat16 [4, 1, 1024, 4, 128], P('pipe', None, 'col', 'row'), may hold values from -6 to 6
- weights: bfloat16 [4, 27, 1024, 1024], P('pipe', None, 'row', 'col'), may hold values from -0.0390625 to 0.0390625
- grad_top: bfloat16 [1, 1024, 4, 128], P(None, 'col', 'row'), may hold values from -6 to 6
Outputs:
- section_grads: bfloat16 [4, 1, 1024, 4, 128], P('pipe', None, 'col', 'row')
- weight_grads: bfloat16 [4, 27, 1024, 1024], P('pipe', None, 'row', 'col')
The draws below stay inside these ranges and needn't reach their ends.
All inputs are finite; a program needn't handle non-finite values.
Results may differ from the reference program's by a relative error of at most 0.02.
Values may be sent and summed in bfloat16 or wider, within the bound.
A program may use at most 128 MiB of HBM per device.

```python
import math
import jax
import jax.numpy as jnp
from jax import lax

C = 1024
BATCH = 1
SY = 8
SZ = 16
CELLS = 128
NX = 4
SECTIONS = 4
N_ROW = 4


def level_of(own_key, extent, shards, smallest, largest):
    loudness, own = 1.0, jax.random.fold_in(own_key, 6)
    for position, parts in shards:
        draws = jnp.exp(jax.random.uniform(jax.random.fold_in(own, position), (parts,), jnp.float32, smallest / len(shards), largest / len(shards)))
        loudness = loudness * jnp.repeat(draws, extent[position] // parts).reshape([-1 if axis == position else 1 for axis in range(len(extent))])
    return loudness


def normal_values(rng, shape, deviation, bound, shards=(), dtype=jnp.bfloat16):
    array = jax.random.normal(rng, shape, jnp.float32) * deviation
    if len(shards) > 0:
        array = level_of(rng, shape, shards, -0.22, 0.18) * array
    return jnp.clip(array, min=-bound, max=bound).astype(dtype)


def setup_inputs(seed: int = 0) -> dict:
    key_of = jax.random.split(jax.random.key(seed), 4)
    acts = normal_values(key_of[0], (SECTIONS, BATCH, C, NX, CELLS), 1.0, 6.0, ((0, 4), (2, 2), (3, 4)))
    weights = normal_values(key_of[1], (SECTIONS, 27, C, C), (27 * C) ** -0.5, 0.0390625, ((0, 4), (2, 4), (3, 2)))
    grad_top = normal_values(key_of[2], (BATCH, C, NX, CELLS), 1.0, 6.0, ((1, 2), (2, 4)))
    return dict(acts=acts, weights=weights, grad_top=grad_top)


tap_offsets = [(shift_x, shift_y, shift_z) for shift_x in (-1, 0, 1) for shift_y in (-1, 0, 1) for shift_z in (-1, 0, 1)]

def shift_grid(field_in, shift_x, shift_y, shift_z):
    padded = jnp.pad(field_in, ((0, 0), (1, 1), (1, 1), (1, 1)))
    return padded[:, 1 + shift_x:1 + shift_x + NX, 1 + shift_y:1 + shift_y + SY, 1 + shift_z:1 + shift_z + SZ]

def reference(acts, weights, grad_top):
    grad_scale = 1.0 / math.sqrt(BATCH * NX * SY * SZ)
    total_cells = NX * SY * SZ
    current = grad_top
    grads_list = [None] * SECTIONS
    kernel_list = [None] * SECTIONS
    for section_index in reversed(range(SECTIONS)):
        tap_sums = [jnp.zeros((C, C), jnp.float32) for tap_index in range(27)]
        lower_all = []
        for sample in range(BATCH):
            inputs = acts[section_index, sample].reshape(C, NX, SY, SZ)
            relu_part = jnp.maximum(inputs, jnp.zeros_like(inputs)).astype(jnp.float32)
            upper_grad = current[sample].reshape(C, NX, SY, SZ).astype(jnp.float32)
            upper_flat = upper_grad.reshape(C, total_cells)
            back_blocks = jnp.zeros((N_ROW, C, total_cells), jnp.float32)
            for tap_index, (shift_x, shift_y, shift_z) in enumerate(tap_offsets):
                kernel = weights[section_index, tap_index].astype(jnp.float32).reshape(N_ROW, C // N_ROW, C)
                moved_grad = shift_grid(upper_grad, -shift_x, -shift_y, -shift_z).reshape(N_ROW, C // N_ROW, total_cells)
                back_blocks = back_blocks + jnp.einsum('rqi,rqp->rip', kernel, moved_grad, precision=lax.Precision.HIGHEST)
                moved_act = shift_grid(relu_part, shift_x, shift_y, shift_z).reshape(C, total_cells)
                tap_sums[tap_index] = tap_sums[tap_index] + jnp.dot(upper_flat, moved_act.T, precision=lax.Precision.HIGHEST)
            rounded = lax.optimization_barrier(back_blocks.astype(jnp.bfloat16))
            back_grad = lax.optimization_barrier(jnp.sum(rounded.astype(jnp.float32), axis=0))
            gate_mask = (inputs > 0).reshape(C, total_cells)
            lower_grad = (upper_flat + jnp.where(gate_mask, back_grad, jnp.zeros_like(back_grad))).astype(jnp.bfloat16)
            lower_all.append(lower_grad.reshape(C, NX, SY * SZ))
        grads_list[section_index] = jnp.stack(lower_all)
        kernel_list[section_index] = (jnp.stack(tap_sums) * grad_scale).astype(jnp.bfloat16)
        current = grads_list[section_index]
    return (jnp.stack(grads_list), jnp.stack(kernel_list))
```

```python
import functools
import math

import jax
import jax.numpy as jnp
from jax import lax
from jax.experimental import pallas as pl
from jax.experimental.pallas import tpu as pltpu
from jax.sharding import PartitionSpec as P

SZ = 16
MESH = pl.DeviceIdType.MESH


def moved_rows(block, shift):
    if shift == 0:
        return block
    wide = block.astype(jnp.float32)
    rows = wide.shape[0]
    rolled = pltpu.roll(wide, shift % rows, axis=0)
    column = lax.broadcasted_iota(jnp.int32, wide.shape, 0) % SZ
    inside = (column - shift >= 0) & (column - shift < SZ)
    return jnp.where(inside, rolled, jnp.zeros_like(rolled)).astype(block.dtype)


def chain_kernel(
    sections, rows, cols, per_col,
    w_hbm, act_ref, top_ref,
    sg_out, gin_out, act_out,
    w_vmem, gin, gbuf, acc, sbuf, pbuf, gout, act_all, sg,
    w_sem, top_send, gin_recv, fwd_send, act_send, act_recv,
    part_send, part_recv, pipe_send, out_send, out_recv,
):
    s, r, c = lax.axis_index("pipe"), lax.axis_index("row"), lax.axis_index("col")
    home = r // per_col
    slot = r % per_col
    cells, width = act_ref.shape[1], act_ref.shape[2]
    is_home = c == home
    is_top = s == sections - 1

    def remote(src, dst, send, recv, **where):
        return pltpu.make_async_remote_copy(
            src_ref=src, dst_ref=dst, send_sem=send, recv_sem=recv,
            device_id=where, device_id_type=MESH,
        )

    w_copy = pltpu.make_async_copy(w_hbm, w_vmem, w_sem)
    w_copy.start()

    barrier = pltpu.get_barrier_semaphore()
    for step in range(1, rows * cols):
        other = lax.rem(r * cols + c + step, rows * cols)
        pl.semaphore_signal(
            barrier, inc=1, device_id={"row": other // cols, "col": other % cols},
            device_id_type=MESH,
        )
    for step in (1, sections - 1):
        pl.semaphore_signal(
            barrier, inc=1, device_id={"pipe": lax.rem(s + step, sections)},
            device_id_type=MESH,
        )
    gbuf[...] = jnp.zeros_like(gbuf)
    pl.semaphore_wait(barrier, rows * cols + 1)

    def top_copy(j, q):
        return remote(
            top_ref.at[j], gin.at[r], top_send.at[j * cols + q], gin_recv.at[r],
            row=c * per_col + j, col=q,
        )

    def top_is_far(j, q):
        return is_top & ~((c * per_col + j == r) & (q == c))

    for j in range(per_col):
        for q in range(cols):
            @pl.when(top_is_far(j, q))
            def _():
                top_copy(j, q).start()

    @pl.when(is_top & is_home)
    def _():
        gin[r] = top_ref[slot]

    def act_copy(row):
        return remote(act_ref, act_all.at[r], act_send.at[row], act_recv.at[r], row=row)

    for row in range(rows):
        @pl.when(row != r)
        def _():
            act_copy(row).start()
    act_all[r] = act_ref[...]

    def fwd_copy(p, q):
        return remote(gin.at[p], gin.at[p], fwd_send.at[p, q], gin_recv.at[p], col=q)

    forwards = is_home & (s < sections - 1)
    for p in range(rows):
        @pl.when(~(is_top & is_home & (p == r)))
        def _():
            remote(gin.at[p], gin.at[p], fwd_send.at[p, 0], gin_recv.at[p], col=c).wait_recv()
        for q in range(cols):
            @pl.when(forwards & (q != c))
            def _():
                fwd_copy(p, q).start()
        for k in range(3):
            gbuf[p + 1, SZ:SZ + cells, k * width:(k + 1) * width] = moved_rows(gin[p], k - 1)

    w_copy.wait()

    def part_copy(j):
        return remote(
            sbuf.at[j], pbuf.at[r], part_send.at[j], part_recv.at[r], row=c * per_col + j,
        )

    for j in range(per_col):
        acc[...] = jnp.zeros_like(acc)

        def tap_plane(t, carry):
            start = pl.multiple_of((2 - t % 3) * SZ, SZ)
            left = gbuf[pl.ds(2 - t // 3, rows), pl.ds(start, cells), :]
            left = left.reshape(rows * cells, 3 * width)
            acc[...] += jnp.dot(
                left, w_vmem[t, :, j * width:(j + 1) * width],
                preferred_element_type=jnp.float32,
            )
            return carry

        lax.fori_loop(0, 9, tap_plane, 0)
        share = acc[...].astype(jnp.bfloat16).reshape(rows, cells, width)
        sbuf[j] = share
        target = c * per_col + j

        @pl.when(target != r)
        def _():
            part_copy(j).start()

        @pl.when(target == r)
        def _():
            pbuf[r] = share

    for row in range(rows):
        @pl.when(row != r)
        def _():
            remote(act_ref, act_all.at[row], act_send.at[row], act_recv.at[row], row=row).wait_recv()

    def pipe_copy(p):
        return remote(gout.at[p], gin.at[p], pipe_send.at[p], gin_recv.at[p], pipe=s - 1)

    def out_copy(p):
        return remote(gout.at[p], sg.at[slot], out_send.at[p], out_recv.at[slot], row=p)

    @pl.when(is_home)
    def _():
        for row in range(rows):
            @pl.when(row != r)
            def _():
                remote(
                    pbuf.at[row], pbuf.at[row], part_send.at[0], part_recv.at[row], row=row
                ).wait_recv()
        for p in range(rows):
            back = pbuf[0, p].astype(jnp.float32)
            for row in range(1, rows):
                back = back + pbuf[row, p].astype(jnp.float32)
            gate = act_all[p, slot] > 0
            fresh = gin[p].astype(jnp.float32) + jnp.where(gate, back, jnp.zeros_like(back))
            gout[p] = fresh.astype(jnp.bfloat16)

            @pl.when(s > 0)
            def _():
                pipe_copy(p).start()

            @pl.when(p != r)
            def _():
                out_copy(p).start()

            @pl.when(p == r)
            def _():
                sg[slot] = gout[p]

    gin_out[...] = gin[...]
    act_out[...] = act_all[...]
    for j in range(per_col):
        @pl.when(c * per_col + j != r)
        def _():
            remote(
                gout.at[0], sg.at[j], out_send.at[0], out_recv.at[j], row=c * per_col + j
            ).wait_recv()
    sg_out[...] = sg[...]

    for j in range(per_col):
        for q in range(cols):
            @pl.when(top_is_far(j, q))
            def _():
                top_copy(j, q).wait_send()

        @pl.when(c * per_col + j != r)
        def _():
            part_copy(j).wait_send()
    for row in range(rows):
        @pl.when(row != r)
        def _():
            act_copy(row).wait_send()
    for p in range(rows):
        for q in range(cols):
            @pl.when(forwards & (q != c))
            def _():
                fwd_copy(p, q).wait_send()

        @pl.when(is_home & (s > 0))
        def _():
            pipe_copy(p).wait_send()

        @pl.when(is_home & (p != r))
        def _():
            out_copy(p).wait_send()


def weight_kernel(scale, gin_ref, act_ref, out_ref, left, field):
    rows, cells, width = gin_ref.shape
    per_col = act_ref.shape[1]

    @pl.when(pl.program_id(0) == 0)
    def _():
        field[...] = jnp.zeros_like(field)
        for p in range(rows):
            left[:, p * cells:(p + 1) * cells] = jnp.transpose(gin_ref[p])
            for j in range(per_col):
                part = jnp.maximum(act_ref[p, j], jnp.zeros_like(act_ref[p, j]))
                for k in range(3):
                    field[k, p + 1, SZ:SZ + cells, j * width:(j + 1) * width] = moved_rows(
                        part, 1 - k
                    )

    t = pl.program_id(0)
    start = pl.multiple_of((t % 3) * SZ, SZ)
    for k in range(3):
        right = field[k, pl.ds(t // 3, rows), pl.ds(start, cells), :]
        right = right.reshape(rows * cells, per_col * width)
        total = jnp.dot(left[...], right, preferred_element_type=jnp.float32)
        out_ref[k] = (total * scale).astype(jnp.bfloat16)


def local(acts, weights, grad_top):
    sections, rows, cols = (lax.axis_size(name) for name in ("pipe", "row", "col"))
    taps, width, depth = weights.shape[1:]
    cells = acts.shape[4]
    per_col = depth // width
    scale = 1.0 / math.sqrt(acts.shape[1] * rows * acts.shape[3] * cells)

    def cells_first(field):
        return jnp.transpose(field.reshape(per_col, width, cells), (0, 2, 1))

    act = cells_first(acts[0, 0])
    top = cells_first(grad_top[0])
    kernel = weights.reshape(taps // 3, 3 * width, depth)
    bf16 = jnp.bfloat16
    vmem = pl.BlockSpec(memory_space=pltpu.VMEM)
    dma = pltpu.SemaphoreType.DMA
    sg, gin, act_all = pl.pallas_call(
        functools.partial(chain_kernel, sections, rows, cols, per_col),
        out_shape=(
            jax.ShapeDtypeStruct((per_col, cells, width), bf16),
            jax.ShapeDtypeStruct((rows, cells, width), bf16),
            jax.ShapeDtypeStruct((rows, per_col, cells, width), bf16),
        ),
        in_specs=[pl.BlockSpec(memory_space=pl.ANY), vmem, vmem],
        out_specs=(vmem, vmem, vmem),
        scratch_shapes=[
            pltpu.VMEM((taps // 3, 3 * width, depth), bf16),
            pltpu.VMEM((rows, cells, width), bf16),
            pltpu.VMEM((rows + 2, cells + 2 * SZ, 3 * width), bf16),
            pltpu.VMEM((rows * cells, width), jnp.float32),
            pltpu.VMEM((per_col, rows, cells, width), bf16),
            pltpu.VMEM((rows, rows, cells, width), bf16),
            pltpu.VMEM((rows, cells, width), bf16),
            pltpu.VMEM((rows, per_col, cells, width), bf16),
            pltpu.VMEM((per_col, cells, width), bf16),
            dma,
            dma((per_col * cols,)),
            dma((rows,)),
            dma((rows, cols)),
            dma((rows,)),
            dma((rows,)),
            dma((per_col,)),
            dma((rows,)),
            dma((rows,)),
            dma((rows,)),
            dma((per_col,)),
        ],
        compiler_params=pltpu.CompilerParams(
            collective_id=0, has_side_effects=True, vmem_limit_bytes=48 * 2**20
        ),
        name="chain",
    )(kernel, act, top)

    weight_grads = pl.pallas_call(
        functools.partial(weight_kernel, scale),
        out_shape=jax.ShapeDtypeStruct((taps, width, depth), bf16),
        grid=(taps // 3,),
        in_specs=[
            pl.BlockSpec((rows, cells, width), lambda t: (0, 0, 0)),
            pl.BlockSpec((rows, per_col, cells, width), lambda t: (0, 0, 0, 0)),
        ],
        out_specs=pl.BlockSpec((3, width, depth), lambda t: (t, 0, 0)),
        scratch_shapes=[
            pltpu.VMEM((width, rows * cells), bf16),
            pltpu.VMEM((3, rows + 2, cells + 2 * SZ, depth), bf16),
        ],
        compiler_params=pltpu.CompilerParams(vmem_limit_bytes=48 * 2**20),
        name="weight",
    )(gin, act_all)
    section_grads = jnp.transpose(sg, (0, 2, 1)).reshape(depth, 1, cells)
    return (section_grads[None, None], weight_grads[None])


def solution(mesh):
    return jax.shard_map(
        local,
        mesh=mesh,
        in_specs=(
            P("pipe", None, "col", "row", None),
            P("pipe", None, "row", "col"),
            P(None, "col", "row", None),
        ),
        out_specs=(P("pipe", None, "col", "row", None), P("pipe", None, "row", "col")),
        check_vma=False,
    )
```

```python
import functools
import math

import jax
import jax.numpy as jnp
from jax import lax
from jax.experimental import pallas as pl
from jax.experimental.pallas import tpu as pltpu
from jax.sharding import PartitionSpec as P

SZ = 16
MESH = pl.DeviceIdType.MESH


def moved_rows(block, shift):
    if shift == 0:
        return block
    wide = block.astype(jnp.float32)
    rows = wide.shape[0]
    rolled = pltpu.roll(wide, shift % rows, axis=0)
    column = lax.broadcasted_iota(jnp.int32, wide.shape, 0) % SZ
    inside = (column - shift >= 0) & (column - shift < SZ)
    return jnp.where(inside, rolled, jnp.zeros_like(rolled)).astype(block.dtype)


def chain_kernel(
    sections, rows, cols, per_col, scale,
    w_hbm, act_in, top_in,
    sg_out, wg_out,
    w_vmem, act_ref, top_ref, gin, gbuf, acc, sbuf, pbuf, gout, act_all, sg, left, field,
    w_sem, top_send, gin_recv, fwd_send, act_send, act_recv,
    part_send, part_recv, pipe_send, out_send, out_recv,
):
    s, r, c = lax.axis_index("pipe"), lax.axis_index("row"), lax.axis_index("col")
    home = r // per_col
    slot = r % per_col
    cells, width = act_ref.shape[1], act_ref.shape[2]
    half = acc.shape[0] // cells
    halves = rows // half
    is_home = c == home
    is_top = s == sections - 1
    is_last = s == 0

    def remote(src, dst, send, recv, **where):
        return pltpu.make_async_remote_copy(
            src_ref=src, dst_ref=dst, send_sem=send, recv_sem=recv,
            device_id=where, device_id_type=MESH,
        )

    w_copy = pltpu.make_async_copy(w_hbm, w_vmem, w_sem)
    w_copy.start()

    barrier = pltpu.get_barrier_semaphore()
    for step in range(1, rows * cols):
        other = lax.rem(r * cols + c + step, rows * cols)
        pl.semaphore_signal(
            barrier, inc=1, device_id={"row": other // cols, "col": other % cols},
            device_id_type=MESH,
        )
    for step in (1, sections - 1):
        pl.semaphore_signal(
            barrier, inc=1, device_id={"pipe": lax.rem(s + step, sections)},
            device_id_type=MESH,
        )
    for j in range(per_col):
        top_ref[j] = jnp.transpose(top_in[j * width:(j + 1) * width])
    for j in range(per_col):
        act_ref[j] = jnp.transpose(act_in[j * width:(j + 1) * width])
    pl.semaphore_wait(barrier, rows * cols + 1)

    def top_copy(j, q):
        return remote(
            top_ref.at[j], gin.at[r], top_send.at[j * cols + q], gin_recv.at[r],
            row=c * per_col + j, col=q,
        )

    def top_is_far(j, q):
        return is_top & ~((c * per_col + j == r) & (q == c))

    for j in range(per_col):
        for q in range(cols):
            @pl.when(top_is_far(j, q))
            def _():
                top_copy(j, q).start()

    @pl.when(is_top & is_home)
    def _():
        gin[r] = top_ref[slot]

    def act_copy(row, j):
        return remote(
            act_ref.at[j], act_all.at[r, j], act_send.at[row, j], act_recv.at[r, j], row=row
        )

    def act_wait(p, j):
        remote(
            act_ref.at[0], act_all.at[p, j], act_send.at[0, 0], act_recv.at[p, j], row=p
        ).wait_recv()

    def send_other_acts():
        for step in range(1, rows):
            row = lax.rem(r + step, rows)
            for j in range(per_col):
                @pl.when(row != c * per_col + j)
                def _():
                    act_copy(row, j).start()

    def build_field():
        for p in range(rows):
            for j in range(per_col):
                part = act_all[p, j]
                part = jnp.maximum(part, jnp.zeros_like(part))
                for k in range(3):
                    field[k, p + 1, SZ:SZ + cells, j * width:(j + 1) * width] = moved_rows(
                        part, 1 - k
                    )

    for j in range(per_col):
        @pl.when(r != c * per_col + j)
        def _():
            act_copy(c * per_col + j, j).start()
    act_all[r] = act_ref[...]
    gbuf[...] = jnp.zeros_like(gbuf)
    field[...] = jnp.zeros_like(field)

    @pl.when(~is_top)
    def _():
        send_other_acts()
        for p in range(rows):
            @pl.when(p != r)
            def _():
                for j in range(per_col):
                    act_wait(p, j)
        build_field()

    def fwd_copy(p, q):
        return remote(gin.at[p], gin.at[p], fwd_send.at[p, q], gin_recv.at[p], col=q)

    forwards = is_home & (s < sections - 1)
    w_copy.wait()
    for p in range(rows):
        @pl.when(~(is_top & is_home & (p == r)))
        def _():
            remote(gin.at[p], gin.at[p], fwd_send.at[p, 0], gin_recv.at[p], col=c).wait_recv()
        for q in range(cols):
            @pl.when(forwards & (q != c))
            def _():
                fwd_copy(p, q).start()
        for k in range(3):
            gbuf[p + 1, SZ:SZ + cells, k * width:(k + 1) * width] = moved_rows(gin[p], k - 1)

    def part_copy(j, h):
        return remote(
            sbuf.at[j, pl.ds(h * half, half)], pbuf.at[r, pl.ds(h * half, half)],
            part_send.at[j, h], part_recv.at[r, h], row=c * per_col + j,
        )

    for h in range(halves):
        for j in range(per_col):
            acc[...] = jnp.zeros_like(acc)

            def tap_plane(t, carry):
                start = pl.multiple_of((2 - t % 3) * SZ, SZ)
                rhs = w_vmem[t, :, j * width:(j + 1) * width]
                lhs = gbuf[pl.ds(2 - t // 3 + h * half, half), pl.ds(start, cells), :]
                acc[...] += jnp.dot(
                    lhs.reshape(half * cells, 3 * width), rhs,
                    preferred_element_type=jnp.float32,
                )
                return carry

            lax.fori_loop(0, 9, tap_plane, 0)
            share = acc[...].astype(jnp.bfloat16).reshape(half, cells, width)
            sbuf[j, h * half:(h + 1) * half] = share
            target = c * per_col + j

            @pl.when(target != r)
            def _():
                part_copy(j, h).start()

            @pl.when(target == r)
            def _():
                pbuf[r, h * half:(h + 1) * half] = share

    def weight_grads():
        for p in range(rows):
            left[:, p * cells:(p + 1) * cells] = jnp.transpose(gin[p])

        def tap_plane(t, carry):
            start = pl.multiple_of((t % 3) * SZ, SZ)
            for k in range(3):
                right = field[k, pl.ds(t // 3, rows), pl.ds(start, cells), :]
                right = right.reshape(rows * cells, per_col * width)
                total = jnp.dot(left[...], right, preferred_element_type=jnp.float32)
                wg_out[3 * t + k] = (total * scale).astype(jnp.bfloat16)
            return carry

        lax.fori_loop(0, 9, tap_plane, 0)

    @pl.when(is_last)
    def _():
        weight_grads()

    @pl.when(is_top)
    def _():
        send_other_acts()

    def pipe_copy(p):
        return remote(gout.at[p], gin.at[p], pipe_send.at[p], gin_recv.at[p], pipe=s - 1)

    def out_copy(p):
        return remote(gout.at[p], sg.at[slot], out_send.at[p], out_recv.at[slot], row=p)

    @pl.when(is_home)
    def _():
        for p in range(rows):
            @pl.when(is_top & (p != r))
            def _():
                act_wait(p, slot)
        for h in range(halves):
            for row in range(rows):
                @pl.when(row != r)
                def _():
                    remote(
                        pbuf.at[row, pl.ds(h * half, half)], pbuf.at[row, pl.ds(h * half, half)],
                        part_send.at[0, 0], part_recv.at[row, h], row=row,
                    ).wait_recv()
            for p in range(h * half, (h + 1) * half):
                back = pbuf[0, p].astype(jnp.float32)
                for row in range(1, rows):
                    back = back + pbuf[row, p].astype(jnp.float32)
                gate = act_all[p, slot] > 0
                fresh = gin[p].astype(jnp.float32) + jnp.where(gate, back, jnp.zeros_like(back))
                gout[p] = fresh.astype(jnp.bfloat16)

                @pl.when(s > 0)
                def _():
                    pipe_copy(p).start()
        for p in range(rows):
            @pl.when(p != r)
            def _():
                out_copy(p).start()
        sg[slot] = gout[r]

    @pl.when(is_top)
    def _():
        for p in range(rows):
            for j in range(per_col):
                @pl.when((p != r) & ~(is_home & (j == slot)))
                def _():
                    act_wait(p, j)
        build_field()

    @pl.when(~is_last)
    def _():
        weight_grads()

    for j in range(per_col):
        @pl.when(c * per_col + j != r)
        def _():
            remote(
                gout.at[0], sg.at[j], out_send.at[0], out_recv.at[j], row=c * per_col + j
            ).wait_recv()
        sg_out[j * width:(j + 1) * width] = jnp.transpose(sg[j])

    for j in range(per_col):
        for q in range(cols):
            @pl.when(top_is_far(j, q))
            def _():
                top_copy(j, q).wait_send()
        for h in range(halves):
            @pl.when(c * per_col + j != r)
            def _():
                part_copy(j, h).wait_send()
    for row in range(rows):
        @pl.when(row != r)
        def _():
            for j in range(per_col):
                act_copy(row, j).wait_send()
    for p in range(rows):
        for q in range(cols):
            @pl.when(forwards & (q != c))
            def _():
                fwd_copy(p, q).wait_send()

        @pl.when(is_home & (s > 0))
        def _():
            pipe_copy(p).wait_send()

        @pl.when(is_home & (p != r))
        def _():
            out_copy(p).wait_send()


def local(acts, weights, grad_top):
    sections, rows, cols = (lax.axis_size(name) for name in ("pipe", "row", "col"))
    taps, width, depth = weights.shape[1:]
    cells = acts.shape[4]
    per_col = depth // width
    half = rows // 2
    scale = 1.0 / math.sqrt(acts.shape[1] * rows * acts.shape[3] * cells)
    kernel = weights.reshape(taps // 3, 3 * width, depth)
    bf16 = jnp.bfloat16
    vmem = pl.BlockSpec(memory_space=pltpu.VMEM)
    dma = pltpu.SemaphoreType.DMA
    section_grads, weight_grads = pl.pallas_call(
        functools.partial(chain_kernel, sections, rows, cols, per_col, scale),
        out_shape=(
            jax.ShapeDtypeStruct((depth, cells), bf16),
            jax.ShapeDtypeStruct((taps, width, depth), bf16),
        ),
        in_specs=[pl.BlockSpec(memory_space=pltpu.HBM), vmem, vmem],
        out_specs=(vmem, vmem),
        scratch_shapes=[
            pltpu.VMEM((taps // 3, 3 * width, depth), bf16),
            pltpu.VMEM((per_col, cells, width), bf16),
            pltpu.VMEM((per_col, cells, width), bf16),
            pltpu.VMEM((rows, cells, width), bf16),
            pltpu.VMEM((rows + 2, cells + 2 * SZ, 3 * width), bf16),
            pltpu.VMEM((half * cells, width), jnp.float32),
            pltpu.VMEM((per_col, rows, cells, width), bf16),
            pltpu.VMEM((rows, rows, cells, width), bf16),
            pltpu.VMEM((rows, cells, width), bf16),
            pltpu.VMEM((rows, per_col, cells, width), bf16),
            pltpu.VMEM((per_col, cells, width), bf16),
            pltpu.VMEM((width, rows * cells), bf16),
            pltpu.VMEM((3, rows + 2, cells + 2 * SZ, depth), bf16),
            dma,
            dma((per_col * cols,)),
            dma((rows,)),
            dma((rows, cols)),
            dma((rows, per_col)),
            dma((rows, per_col)),
            dma((per_col, 2)),
            dma((rows, 2)),
            dma((rows,)),
            dma((rows,)),
            dma((per_col,)),
        ],
        compiler_params=pltpu.CompilerParams(
            collective_id=0, has_side_effects=True, vmem_limit_bytes=36 * 2**20
        ),
        name="chain",
    )(kernel, acts.reshape(depth, cells), grad_top.reshape(depth, cells))
    return (section_grads.reshape(acts.shape), weight_grads[None])


def solution(mesh):
    return jax.shard_map(
        local,
        mesh=mesh,
        in_specs=(
            P("pipe", None, "col", "row", None),
            P("pipe", None, "row", "col"),
            P(None, "col", "row", None),
        ),
        out_specs=(P("pipe", None, "col", "row", None), P("pipe", None, "row", "col")),
        check_vma=False,
    )
```

```python
import functools
import math

import jax
import jax.numpy as jnp
from jax import lax
from jax.experimental import pallas as pl
from jax.experimental.pallas import tpu as pltpu
from jax.sharding import PartitionSpec as P

SZ = 16
MESH = pl.DeviceIdType.MESH


def moved_rows(block, shift):
    if shift == 0:
        return block
    wide = block.astype(jnp.float32)
    rows = wide.shape[0]
    rolled = pltpu.roll(wide, shift % rows, axis=0)
    column = lax.broadcasted_iota(jnp.int32, wide.shape, 0) % SZ
    inside = (column - shift >= 0) & (column - shift < SZ)
    return jnp.where(inside, rolled, jnp.zeros_like(rolled)).astype(block.dtype)


def chain_kernel(
    sections, rows, cols, per_col, scale,
    w_hbm, act_in, top_in,
    sg_out, wg_out,
    w_vmem, act_ref, top_ref, gin, gbuf, acc, sbuf, pbuf, gout, act_all, sg, left, field,
    w_sem, top_send, gin_recv, fwd_send, act_send, act_recv,
    part_send, part_recv, pipe_send, out_send, out_recv,
):
    s, r, c = lax.axis_index("pipe"), lax.axis_index("row"), lax.axis_index("col")
    home = r // per_col
    slot = r % per_col
    cells, width = act_ref.shape[1], act_ref.shape[2]
    half = acc.shape[0] // cells
    halves = rows // half
    is_home = c == home
    is_top = s == sections - 1
    is_last = s == 0

    def remote(src, dst, send, recv, **where):
        return pltpu.make_async_remote_copy(
            src_ref=src, dst_ref=dst, send_sem=send, recv_sem=recv,
            device_id=where, device_id_type=MESH,
        )

    w_copy = pltpu.make_async_copy(w_hbm, w_vmem, w_sem)
    w_copy.start()

    barrier = pltpu.get_barrier_semaphore()
    partners = [("row", r, step, rows) for step in range(1, rows)]
    partners += [("col", c, step, cols) for step in range(1, cols)]
    partners += [("pipe", s, step, sections) for step in (1, sections - 1)]
    for axis, own, step, size in partners:
        pl.semaphore_signal(
            barrier, inc=1, device_id={axis: lax.rem(own + step, size)}, device_id_type=MESH
        )
    for j in range(per_col):
        top_ref[j] = jnp.transpose(top_in[j * width:(j + 1) * width])
    pl.semaphore_wait(barrier, len(partners))

    def top_copy(j):
        return remote(
            top_ref.at[j], gin.at[r], top_send.at[j], gin_recv.at[r], row=c * per_col + j
        )

    for j in range(per_col):
        @pl.when(is_top & (c * per_col + j != r))
        def _():
            top_copy(j).start()
    for j in range(per_col):
        act_ref[j] = jnp.transpose(act_in[j * width:(j + 1) * width])

    @pl.when(is_top & is_home)
    def _():
        gin[r] = top_ref[slot]

    def act_copy(row, j):
        return remote(
            act_ref.at[j], act_all.at[r, j], act_send.at[row, j], act_recv.at[r, j], row=row
        )

    def act_wait(p, j):
        remote(
            act_ref.at[0], act_all.at[p, j], act_send.at[0, 0], act_recv.at[p, j], row=p
        ).wait_recv()

    def send_other_acts():
        for step in range(1, rows):
            row = lax.rem(r + step, rows)
            for j in range(per_col):
                @pl.when(row != c * per_col + j)
                def _():
                    act_copy(row, j).start()

    def build_field():
        field[...] = jnp.zeros_like(field)
        for p in range(rows):
            for j in range(per_col):
                part = act_all[p, j]
                part = jnp.maximum(part, jnp.zeros_like(part))
                for k in range(3):
                    field[k, p + 1, SZ:SZ + cells, j * width:(j + 1) * width] = moved_rows(
                        part, 1 - k
                    )

    for j in range(per_col):
        @pl.when(r != c * per_col + j)
        def _():
            act_copy(c * per_col + j, j).start()
    act_all[r] = act_ref[...]
    gbuf[...] = jnp.zeros_like(gbuf)

    @pl.when(~is_top)
    def _():
        send_other_acts()
        for p in range(rows):
            @pl.when(p != r)
            def _():
                for j in range(per_col):
                    act_wait(p, j)
        build_field()

    def fwd_copy(p, q):
        return remote(gin.at[p], gin.at[p], fwd_send.at[p, q], gin_recv.at[p], col=q)

    def take_plane(p):
        @pl.when(~(is_top & is_home & (p == r)))
        def _():
            remote(gin.at[p], gin.at[p], fwd_send.at[p, 0], gin_recv.at[p], col=c).wait_recv()
        for q in range(cols):
            @pl.when(is_home & (q != c))
            def _():
                fwd_copy(p, q).start()
        for k in range(3):
            gbuf[p + 1, SZ:SZ + cells, k * width:(k + 1) * width] = moved_rows(gin[p], k - 1)

    def part_copy(j, p):
        return remote(
            sbuf.at[j, p], pbuf.at[r, p], part_send.at[j, p], part_recv.at[r, p],
            row=c * per_col + j,
        )

    def send_shares(j, planes):
        @pl.when(c * per_col + j != r)
        def _():
            for p in planes:
                part_copy(j, p).start()

        @pl.when(c * per_col + j == r)
        def _():
            for p in planes:
                pbuf[r, p] = sbuf[j, p]

    w_copy.wait()
    taken = 0
    for h in range(halves):
        needed = min(rows, (h + 1) * half + 1)
        for p in range(taken, needed):
            take_plane(p)
        taken = needed
        planes = list(range(h * half, (h + 1) * half))
        late = planes[-1:] if h == halves - 1 else []
        for j in range(per_col):
            acc[...] = jnp.zeros_like(acc)

            def tap_plane(t, carry):
                start = pl.multiple_of((2 - t % 3) * SZ, SZ)
                rhs = w_vmem[t, :, j * width:(j + 1) * width]
                lhs = gbuf[pl.ds(2 - t // 3 + h * half, half), pl.ds(start, cells), :]
                acc[...] += jnp.dot(
                    lhs.reshape(half * cells, 3 * width), rhs,
                    preferred_element_type=jnp.float32,
                )
                return carry

            lax.fori_loop(0, 9, tap_plane, 0)
            share = acc[...].astype(jnp.bfloat16).reshape(half, cells, width)
            sbuf[j, h * half:(h + 1) * half] = share
            send_shares(j, [p for p in planes if p not in late])
        for j in range(per_col):
            send_shares(j, late)

    def weight_grads():
        for p in range(rows):
            left[:, p * cells:(p + 1) * cells] = jnp.transpose(gin[p])

        def tap_plane(t, carry):
            start = pl.multiple_of((t % 3) * SZ, SZ)
            for k in range(3):
                right = field[k, pl.ds(t // 3, rows), pl.ds(start, cells), :]
                right = right.reshape(rows * cells, per_col * width)
                total = jnp.dot(left[...], right, preferred_element_type=jnp.float32)
                wg_out[3 * t + k] = (total * scale).astype(jnp.bfloat16)
            return carry

        lax.fori_loop(0, 9, tap_plane, 0)

    @pl.when(is_last)
    def _():
        weight_grads()

    def pipe_copy(p):
        return remote(gout.at[p], gin.at[p], pipe_send.at[p], gin_recv.at[p], pipe=s - 1)

    def out_copy(p):
        return remote(gout.at[p], sg.at[slot], out_send.at[p], out_recv.at[slot], row=p)

    @pl.when(is_home)
    def _():
        for p in range(rows):
            @pl.when(is_top & (p != r))
            def _():
                act_wait(p, slot)
        for p in range(rows):
            for row in range(rows):
                @pl.when(row != r)
                def _():
                    remote(
                        pbuf.at[row, p], pbuf.at[row, p], part_send.at[0, 0],
                        part_recv.at[row, p], row=row,
                    ).wait_recv()
            back = pbuf[0, p].astype(jnp.float32)
            for row in range(1, rows):
                back = back + pbuf[row, p].astype(jnp.float32)
            gate = act_all[p, slot] > 0
            fresh = gin[p].astype(jnp.float32) + jnp.where(gate, back, jnp.zeros_like(back))
            gout[p] = fresh.astype(jnp.bfloat16)

            @pl.when(s > 0)
            def _():
                pipe_copy(p).start()
        for p in range(rows):
            @pl.when(p != r)
            def _():
                out_copy(p).start()
        sg[slot] = gout[r]

    for j in range(per_col):
        @pl.when(c * per_col + j != r)
        def _():
            remote(
                gout.at[0], sg.at[j], out_send.at[0], out_recv.at[j], row=c * per_col + j
            ).wait_recv()
        sg_out[j * width:(j + 1) * width] = jnp.transpose(sg[j])

    @pl.when(is_top)
    def _():
        send_other_acts()
        for p in range(rows):
            for j in range(per_col):
                @pl.when((p != r) & ~(is_home & (j == slot)))
                def _():
                    act_wait(p, j)
        build_field()

    @pl.when(~is_last)
    def _():
        weight_grads()

    for j in range(per_col):
        @pl.when(is_top & (c * per_col + j != r))
        def _():
            top_copy(j).wait_send()

        @pl.when(c * per_col + j != r)
        def _():
            for p in range(rows):
                part_copy(j, p).wait_send()
    for row in range(rows):
        @pl.when(row != r)
        def _():
            for j in range(per_col):
                act_copy(row, j).wait_send()
    for p in range(rows):
        for q in range(cols):
            @pl.when(is_home & (q != c))
            def _():
                fwd_copy(p, q).wait_send()

        @pl.when(is_home & (s > 0))
        def _():
            pipe_copy(p).wait_send()

        @pl.when(is_home & (p != r))
        def _():
            out_copy(p).wait_send()


def local(acts, weights, grad_top):
    sections, rows, cols = (lax.axis_size(name) for name in ("pipe", "row", "col"))
    taps, width, depth = weights.shape[1:]
    cells = acts.shape[4]
    per_col = depth // width
    half = rows // 2
    scale = 1.0 / math.sqrt(acts.shape[1] * rows * acts.shape[3] * cells)
    kernel = weights.reshape(taps // 3, 3 * width, depth)
    bf16 = jnp.bfloat16
    vmem = pl.BlockSpec(memory_space=pltpu.VMEM)
    dma = pltpu.SemaphoreType.DMA
    section_grads, weight_grads = pl.pallas_call(
        functools.partial(chain_kernel, sections, rows, cols, per_col, scale),
        out_shape=(
            jax.ShapeDtypeStruct((depth, cells), bf16),
            jax.ShapeDtypeStruct((taps, width, depth), bf16),
        ),
        in_specs=[pl.BlockSpec(memory_space=pltpu.HBM), vmem, vmem],
        out_specs=(vmem, vmem),
        scratch_shapes=[
            pltpu.VMEM((taps // 3, 3 * width, depth), bf16),
            pltpu.VMEM((per_col, cells, width), bf16),
            pltpu.VMEM((per_col, cells, width), bf16),
            pltpu.VMEM((rows, cells, width), bf16),
            pltpu.VMEM((rows + 2, cells + 2 * SZ, 3 * width), bf16),
            pltpu.VMEM((half * cells, width), jnp.float32),
            pltpu.VMEM((per_col, rows, cells, width), bf16),
            pltpu.VMEM((rows, rows, cells, width), bf16),
            pltpu.VMEM((rows, cells, width), bf16),
            pltpu.VMEM((rows, per_col, cells, width), bf16),
            pltpu.VMEM((per_col, cells, width), bf16),
            pltpu.VMEM((width, rows * cells), bf16),
            pltpu.VMEM((3, rows + 2, cells + 2 * SZ, depth), bf16),
            dma,
            dma((per_col,)),
            dma((rows,)),
            dma((rows, cols)),
            dma((rows, per_col)),
            dma((rows, per_col)),
            dma((per_col, rows)),
            dma((rows, rows)),
            dma((rows,)),
            dma((rows,)),
            dma((per_col,)),
        ],
        compiler_params=pltpu.CompilerParams(
            collective_id=0, has_side_effects=True, vmem_limit_bytes=44 * 2**20
        ),
        name="chain",
    )(kernel, acts.reshape(depth, cells), grad_top.reshape(depth, cells))
    return (section_grads.reshape(acts.shape), weight_grads[None])


def solution(mesh):
    return jax.shard_map(
        local,
        mesh=mesh,
        in_specs=(
            P("pipe", None, "col", "row", None),
            P("pipe", None, "row", "col"),
            P(None, "col", "row", None),
        ),
        out_specs=(P("pipe", None, "col", "row", None), P("pipe", None, "row", "col")),
        check_vma=False,
    )
```

```python
import functools
import math

import jax
import jax.numpy as jnp
from jax import lax
from jax.experimental import pallas as pl
from jax.experimental.pallas import tpu as pltpu
from jax.sharding import PartitionSpec as P

SZ = 16
MESH = pl.DeviceIdType.MESH


def moved_rows(block, shift):
    if shift == 0:
        return block
    wide = block.astype(jnp.float32)
    rows = wide.shape[0]
    rolled = pltpu.roll(wide, shift % rows, axis=0)
    column = lax.broadcasted_iota(jnp.int32, wide.shape, 0) % SZ
    inside = (column - shift >= 0) & (column - shift < SZ)
    return jnp.where(inside, rolled, jnp.zeros_like(rolled)).astype(block.dtype)


def chain_kernel(
    sections, rows, cols, per_col, scale,
    w_hbm, act_in, top_in,
    sg_out, wg_out,
    w_vmem, act_ref, top_ref, gin, gbuf, acc, sbuf, pbuf, gout, act_all, sg, left, field,
    w_sem, top_send, gin_recv, fwd_send, act_send, act_recv,
    part_send, part_recv, pipe_send, out_send, out_recv,
):
    s, r, c = lax.axis_index("pipe"), lax.axis_index("row"), lax.axis_index("col")
    home = r // per_col
    slot = r % per_col
    cells, width = act_ref.shape[1], act_ref.shape[2]
    half = acc.shape[0] // cells
    halves = rows // half
    is_home = c == home
    is_top = s == sections - 1
    is_last = s == 0

    def remote(src, dst, send, recv, **where):
        return pltpu.make_async_remote_copy(
            src_ref=src, dst_ref=dst, send_sem=send, recv_sem=recv,
            device_id=where, device_id_type=MESH,
        )

    w_copy = pltpu.make_async_copy(w_hbm, w_vmem, w_sem)
    w_copy.start()

    barrier = pltpu.get_barrier_semaphore()
    partners = [("row", r, step, rows) for step in range(1, rows)]
    partners += [("col", c, step, cols) for step in range(1, cols)]
    partners += [("pipe", s, step, sections) for step in (1, sections - 1)]
    for axis, own, step, size in partners:
        pl.semaphore_signal(
            barrier, inc=1, device_id={axis: lax.rem(own + step, size)}, device_id_type=MESH
        )
    for j in range(per_col):
        top_ref[j] = jnp.transpose(top_in[j * width:(j + 1) * width])
    pl.semaphore_wait(barrier, len(partners))

    def top_copy(j):
        return remote(
            top_ref.at[j], gin.at[r], top_send.at[j], gin_recv.at[r], row=c * per_col + j
        )

    for j in range(per_col):
        @pl.when(is_top & (c * per_col + j != r))
        def _():
            top_copy(j).start()
    for j in range(per_col):
        act_ref[j] = jnp.transpose(act_in[j * width:(j + 1) * width])

    @pl.when(is_top & is_home)
    def _():
        gin[r] = top_ref[slot]

    def act_copy(row, j):
        return remote(
            act_ref.at[j], act_all.at[r, j], act_send.at[row, j], act_recv.at[r, j], row=row
        )

    def act_wait(p, j):
        remote(
            act_ref.at[0], act_all.at[p, j], act_send.at[0, 0], act_recv.at[p, j], row=p
        ).wait_recv()

    def send_other_acts():
        for step in range(1, rows):
            row = lax.rem(r + step, rows)
            for j in range(per_col):
                @pl.when(row != c * per_col + j)
                def _():
                    act_copy(row, j).start()

    def build_field():
        field[...] = jnp.zeros_like(field)
        for p in range(rows):
            for j in range(per_col):
                part = act_all[p, j]
                part = jnp.maximum(part, jnp.zeros_like(part))
                for k in range(3):
                    field[k, p + 1, SZ:SZ + cells, j * width:(j + 1) * width] = moved_rows(
                        part, 1 - k
                    )

    for j in range(per_col):
        @pl.when(r != c * per_col + j)
        def _():
            act_copy(c * per_col + j, j).start()
    act_all[r] = act_ref[...]
    gbuf[...] = jnp.zeros_like(gbuf)

    @pl.when(~is_top)
    def _():
        send_other_acts()
        for p in range(rows):
            @pl.when(p != r)
            def _():
                for j in range(per_col):
                    act_wait(p, j)
        build_field()

    def fwd_copy(p, q):
        return remote(gin.at[p], gin.at[p], fwd_send.at[p, q], gin_recv.at[p], col=q)

    def take_plane(p):
        @pl.when(~(is_top & is_home & (p == r)))
        def _():
            remote(gin.at[p], gin.at[p], fwd_send.at[p, 0], gin_recv.at[p], col=c).wait_recv()
        for q in range(cols):
            @pl.when(is_home & (q != c))
            def _():
                fwd_copy(p, q).start()
        for k in range(3):
            gbuf[p + 1, SZ:SZ + cells, k * width:(k + 1) * width] = moved_rows(gin[p], k - 1)

    def part_copy(j, p):
        return remote(
            sbuf.at[j, p], pbuf.at[r, p], part_send.at[j, p], part_recv.at[r, p],
            row=c * per_col + j,
        )

    def send_shares(j, planes):
        @pl.when(c * per_col + j != r)
        def _():
            for p in planes:
                part_copy(j, p).start()

        @pl.when(c * per_col + j == r)
        def _():
            for p in planes:
                pbuf[r, p] = sbuf[j, p]

    w_copy.wait()
    taken = 0
    for h in range(halves):
        needed = min(rows, (h + 1) * half + 1)
        for p in range(taken, needed):
            take_plane(p)
        taken = needed
        planes = list(range(h * half, (h + 1) * half))
        late = planes[-1:] if h == halves - 1 else []
        for j in range(per_col):
            acc[...] = jnp.zeros_like(acc)

            def tap_plane(t, carry):
                start = pl.multiple_of((2 - t % 3) * SZ, SZ)
                rhs = w_vmem[t, :, j * width:(j + 1) * width]
                lhs = gbuf[pl.ds(2 - t // 3 + h * half, half), pl.ds(start, cells), :]
                acc[...] += jnp.dot(
                    lhs.reshape(half * cells, 3 * width), rhs,
                    preferred_element_type=jnp.float32,
                )
                return carry

            lax.fori_loop(0, 9, tap_plane, 0, unroll=3)
            share = acc[...].astype(jnp.bfloat16).reshape(half, cells, width)
            sbuf[j, h * half:(h + 1) * half] = share
            send_shares(j, [p for p in planes if p not in late])
        for j in range(per_col):
            send_shares(j, late)

    def turn_grads():
        for p in range(rows):
            left[:, p * cells:(p + 1) * cells] = jnp.transpose(gin[p])

    def weight_grads(first, last):
        def tap_plane(t, carry):
            start = pl.multiple_of((t % 3) * SZ, SZ)
            for k in range(3):
                right = field[k, pl.ds(t // 3, rows), pl.ds(start, cells), :]
                right = right.reshape(rows * cells, per_col * width)
                total = jnp.dot(left[...], right, preferred_element_type=jnp.float32)
                wg_out[3 * t + k] = (total * scale).astype(jnp.bfloat16)
            return carry

        lax.fori_loop(first, last, tap_plane, 0)

    @pl.when(is_last)
    def _():
        turn_grads()
        weight_grads(0, 5)

    def pipe_copy(p):
        return remote(gout.at[p], gin.at[p], pipe_send.at[p], gin_recv.at[p], pipe=s - 1)

    def out_copy(p):
        return remote(gout.at[p], sg.at[slot], out_send.at[p], out_recv.at[slot], row=p)

    @pl.when(is_home)
    def _():
        for p in range(rows):
            @pl.when(is_top & (p != r))
            def _():
                act_wait(p, slot)
        for p in range(rows):
            for row in range(rows):
                @pl.when(row != r)
                def _():
                    remote(
                        pbuf.at[row, p], pbuf.at[row, p], part_send.at[0, 0],
                        part_recv.at[row, p], row=row,
                    ).wait_recv()
            back = pbuf[0, p].astype(jnp.float32)
            for row in range(1, rows):
                back = back + pbuf[row, p].astype(jnp.float32)
            gate = act_all[p, slot] > 0
            fresh = gin[p].astype(jnp.float32) + jnp.where(gate, back, jnp.zeros_like(back))
            gout[p] = fresh.astype(jnp.bfloat16)

            @pl.when(s > 0)
            def _():
                pipe_copy(p).start()
        for p in range(rows):
            @pl.when(p != r)
            def _():
                out_copy(p).start()
        sg[slot] = gout[r]

    @pl.when(is_last)
    def _():
        weight_grads(5, 9)

    for j in range(per_col):
        @pl.when(c * per_col + j != r)
        def _():
            remote(
                gout.at[0], sg.at[j], out_send.at[0], out_recv.at[j], row=c * per_col + j
            ).wait_recv()
        sg_out[j * width:(j + 1) * width] = jnp.transpose(sg[j])

    @pl.when(is_top)
    def _():
        send_other_acts()
        for p in range(rows):
            for j in range(per_col):
                @pl.when((p != r) & ~(is_home & (j == slot)))
                def _():
                    act_wait(p, j)
        build_field()

    @pl.when(~is_last)
    def _():
        turn_grads()
        weight_grads(0, 9)

    for j in range(per_col):
        @pl.when(is_top & (c * per_col + j != r))
        def _():
            top_copy(j).wait_send()

        @pl.when(c * per_col + j != r)
        def _():
            for p in range(rows):
                part_copy(j, p).wait_send()
    for row in range(rows):
        @pl.when(row != r)
        def _():
            for j in range(per_col):
                act_copy(row, j).wait_send()
    for p in range(rows):
        for q in range(cols):
            @pl.when(is_home & (q != c))
            def _():
                fwd_copy(p, q).wait_send()

        @pl.when(is_home & (s > 0))
        def _():
            pipe_copy(p).wait_send()

        @pl.when(is_home & (p != r))
        def _():
            out_copy(p).wait_send()


def local(acts, weights, grad_top):
    sections, rows, cols = (lax.axis_size(name) for name in ("pipe", "row", "col"))
    taps, width, depth = weights.shape[1:]
    cells = acts.shape[4]
    per_col = depth // width
    half = rows // 2
    scale = 1.0 / math.sqrt(acts.shape[1] * rows * acts.shape[3] * cells)
    kernel = weights.reshape(taps // 3, 3 * width, depth)
    bf16 = jnp.bfloat16
    vmem = pl.BlockSpec(memory_space=pltpu.VMEM)
    dma = pltpu.SemaphoreType.DMA
    section_grads, weight_grads = pl.pallas_call(
        functools.partial(chain_kernel, sections, rows, cols, per_col, scale),
        out_shape=(
            jax.ShapeDtypeStruct((depth, cells), bf16),
            jax.ShapeDtypeStruct((taps, width, depth), bf16),
        ),
        in_specs=[pl.BlockSpec(memory_space=pltpu.HBM), vmem, vmem],
        out_specs=(vmem, vmem),
        scratch_shapes=[
            pltpu.VMEM((taps // 3, 3 * width, depth), bf16),
            pltpu.VMEM((per_col, cells, width), bf16),
            pltpu.VMEM((per_col, cells, width), bf16),
            pltpu.VMEM((rows, cells, width), bf16),
            pltpu.VMEM((rows + 2, cells + 2 * SZ, 3 * width), bf16),
            pltpu.VMEM((half * cells, width), jnp.float32),
            pltpu.VMEM((per_col, rows, cells, width), bf16),
            pltpu.VMEM((rows, rows, cells, width), bf16),
            pltpu.VMEM((rows, cells, width), bf16),
            pltpu.VMEM((rows, per_col, cells, width), bf16),
            pltpu.VMEM((per_col, cells, width), bf16),
            pltpu.VMEM((width, rows * cells), bf16),
            pltpu.VMEM((3, rows + 2, cells + 2 * SZ, depth), bf16),
            dma,
            dma((per_col,)),
            dma((rows,)),
            dma((rows, cols)),
            dma((rows, per_col)),
            dma((rows, per_col)),
            dma((per_col, rows)),
            dma((rows, rows)),
            dma((rows,)),
            dma((rows,)),
            dma((per_col,)),
        ],
        compiler_params=pltpu.CompilerParams(
            collective_id=0, has_side_effects=True, vmem_limit_bytes=44 * 2**20
        ),
        name="chain",
    )(kernel, acts.reshape(depth, cells), grad_top.reshape(depth, cells))
    return (section_grads.reshape(acts.shape), weight_grads[None])


def solution(mesh):
    return jax.shard_map(
        local,
        mesh=mesh,
        in_specs=(
            P("pipe", None, "col", "row", None),
            P("pipe", None, "row", "col"),
            P(None, "col", "row", None),
        ),
        out_specs=(P("pipe", None, "col", "row", None), P("pipe", None, "row", "col")),
        check_vma=False,
    )
```
